32 devices in a mesh: grp: 4 (over x, core), mem: 8 (over z, y).
Axes of the slice: x: 2, y: 2, z: 4, core: 2. Of those that a mesh axis runs over, the one named last changes fastest.
Arguments:
- history: bfloat16 [16384, 256], P(('grp', 'mem')), may hold values from -6 to 6
- tiles: bfloat16 [20480, 128, 128], P(('grp', 'mem')), may hold values from -0.0390625 to 0.0390625
- tile_row: int32 [20480], P(('grp', 'mem')), may hold values from 0 to 31
- tile_col: int32 [20480], P(('grp', 'mem')), may hold values from 0 to 31
- weight: bfloat16 [256, 256], replicated, may hold values from -0.375 to 0.375
- bias: float32 [256], replicated, may hold values from -3 to 3
- cotangent: bfloat16 [16384, 256], P(('grp', 'mem')), may hold values from -0.046875 to 0.046875
Outputs:
- activation: bfloat16 [16384, 256], P(('grp', 'mem'))
- weight_grad: float32 [256, 256], replicated
- bias_grad: float32 [256], replicated
The draws below stay inside these ranges and needn't reach their ends.
All inputs are finite; a program needn't handle non-finite values.
Results may differ from the reference program's by a relative error of at most 0.012.
Values may be sent and summed in bfloat16 or wider, within the bound.
No kernel may reach another device: no remote copies, remote signals or barrier semaphores. Data moves between devices by JAX's collectives and lax.ppermute only.
A program may use at most 128 MiB of HBM per device.

```python
import math
import jax
import jax.numpy as jnp
import numpy as np
from jax import lax

H = 256
BS = 128
RB = 4
TILE_DEV = 640
NODES = 16384
TILES = 20480
N_GRP = 4
N_MEM = 8


def plant(result, rng, low, largest):
    longest = result.shape.index(max(result.shape))
    spots = []
    for shift in (0, 1):
        where = [jax.random.randint(jax.random.fold_in(rng, axis), (), 0, length) for axis, length in enumerate(result.shape)]
        where[longest] = (where[longest] + shift) % result.shape[longest]
        spots.append(tuple(where))
    return result.at[spots[0]].set(low).at[spots[1]].set(largest)


def block_scale(rng, extent, cuts, low, largest):
    loudness = 1.0
    for dim, shards_of in cuts:
        steps = jax.random.uniform(jax.random.fold_in(jax.random.fold_in(rng, 6), dim), (shards_of,), jnp.float32, low / len(cuts), largest / len(cuts))
        loudness = loudness * jnp.repeat(jnp.exp(steps), extent[dim] // shards_of).reshape((-1,) + (1,) * (len(extent) - 1 - dim))
    return loudness


def cumulative_ranks(amount, skew):
    weights = [(1 << 20) // math.isqrt(standing ** skew) + 1 for standing in range(1, amount + 1)]
    scale = 1 + sum(weights) // (1 << 30)
    return np.cumsum(np.array([max(1, weight // scale) for weight in weights]))


def skewed_ids(key, extent, amount, lean):
    listing = cumulative_ranks(amount, lean)
    lot = jax.random.randint(jax.random.fold_in(key, 1), extent, 0, int(listing[amount - 1]))
    standing = jnp.searchsorted(jnp.asarray(listing, jnp.int32), lot, side="right")
    return jax.random.permutation(jax.random.fold_in(key, 2), amount)[standing].astype(jnp.int32)


def bell_draw(stream_key, extent, width, bound, cuts=(), held_as=jnp.bfloat16):
    gain = block_scale(stream_key, extent, cuts, -0.22, 0.18) if cuts else 1.0
    array = jax.random.normal(stream_key, extent, jnp.float32) * width * gain
    return jnp.minimum(jnp.maximum(array, -bound), bound).astype(held_as)


def setup_inputs(seed: int = 0) -> dict:
    key_of = jax.random.split(jax.random.key(seed), 8)
    return {
        "history": bell_draw(key_of[0], (NODES, H), 1.0, 6.0, ((0, 32),)),
        "tiles": bell_draw(key_of[1], (TILES, BS, BS), (TILE_DEV * BS // RB) ** -0.5, 0.0390625, ((0, 32),)),
        "tile_row": plant(skewed_ids(key_of[2], (TILES,), RB * N_MEM, 2), jax.random.fold_in(key_of[2], 3), 0, (RB * N_MEM) - 1).astype(jnp.int32),
        "tile_col": plant(jax.random.randint(key_of[3], (TILES,), 0, RB * N_MEM), jax.random.fold_in(key_of[3], 1), 0, (RB * N_MEM) - 1).astype(jnp.int32),
        "weight": bell_draw(key_of[4], (H, H), H ** -0.5, 0.375),
        "bias": bell_draw(key_of[5], (H,), 0.5, 3.0, (), jnp.float32),
        "cotangent": bell_draw(key_of[6], (NODES, H), (1.0 / NODES ** 0.5), 0.046875, ((0, 32),)),
    }


def reference(history, tiles, tile_row, tile_col, weight, bias, cotangent):
    nblk = N_MEM * RB
    hist = history.reshape(N_GRP, nblk, BS, H)
    group_tiles = tiles.reshape(N_GRP, N_MEM * TILE_DEV, BS, BS)
    rows_all = tile_row.reshape(N_GRP, N_MEM * TILE_DEV)
    cols_all = tile_col.reshape(N_GRP, N_MEM * TILE_DEV)
    step = math.gcd(TILE_DEV, 64)
    count = (N_MEM * TILE_DEV) // step

    def one_group(items):
        blocks, gtiles, grows, gcols = items

        def accumulate(dense, index):
            start = (index * step).astype(jnp.int32)
            piece = lax.dynamic_slice_in_dim(gtiles, start, step, 0).astype(jnp.float32)
            rows = lax.dynamic_slice_in_dim(grows, start, step, 0)
            cols = lax.dynamic_slice_in_dim(gcols, start, step, 0)
            picked = blocks[cols].astype(jnp.float32)
            part = jnp.einsum("tij,tjh->tih", piece, picked, precision=lax.Precision.HIGHEST)
            return dense + jax.ops.segment_sum(part, rows, num_segments=nblk), None

        dense, unused = lax.scan(accumulate, jnp.zeros((nblk, BS, H), jnp.float32), jnp.arange(count, dtype=jnp.int32))
        return dense

    dense = lax.map(one_group, (hist, group_tiles, rows_all, cols_all))
    merged = dense.reshape(NODES, H).astype(jnp.bfloat16)
    pre = jnp.dot(merged, weight, preferred_element_type=jnp.float32) + bias
    sig = jax.nn.sigmoid(pre)
    activation = (pre * sig).astype(jnp.bfloat16)
    slope = sig * (1.0 + pre * (1.0 - sig))
    masked = (cotangent.astype(jnp.float32) * slope).astype(jnp.bfloat16)
    weight_grad = jnp.dot(merged.T, masked, preferred_element_type=jnp.float32)
    bias_grad = jnp.sum(masked.astype(jnp.float32), axis=0)
    return activation, weight_grad, bias_grad
```

```python
import functools

import jax
import jax.numpy as jnp
from jax import lax
from jax.experimental import pallas as pl
from jax.experimental.pallas import tpu as pltpu
from jax.sharding import PartitionSpec as P

G = 4
U = 8
NCOPY = 20
F32 = jnp.float32
BF16 = jnp.bfloat16


def swap(value, axis, size, mask):
    return lax.ppermute(value, axis, [(i, i ^ mask) for i in range(size)])


def plan(row, col, me, rb, nblk, nchunk):
    nt = row.shape[0]
    rel_row = ((row // rb) ^ me) * rb + row % rb
    rel_col = ((col // rb) ^ me) * rb + col % rb
    tile = jnp.arange(nt, dtype=jnp.int32)
    blocks = jnp.arange(nblk, dtype=jnp.int32)
    per_chunk = nblk // nchunk
    counts = jnp.sum((rel_row[None, :] == blocks[:, None]).astype(jnp.int32), axis=1)
    padded = (counts + (G - 1)) // G * G
    same_chunk = (blocks[:, None] // per_chunk) == (blocks[None, :] // per_chunk)
    before = blocks[None, :] < blocks[:, None]
    within = jnp.sum(jnp.where(same_chunk & before, padded[None, :], 0), axis=1)
    chunks = jnp.arange(nchunk, dtype=jnp.int32)
    totals = jnp.sum(
        jnp.where(chunks[:, None] == blocks[None, :] // per_chunk, padded[None, :], 0), axis=1
    )
    steps = (totals + (G * U - 1)) // (G * U)
    first = jnp.sum(jnp.where(chunks[None, :] < chunks[:, None], steps[None, :], 0), axis=1)
    chunk_of = blocks // per_chunk
    base = within + G * U * jnp.sum(
        jnp.where(chunk_of[:, None] == chunks[None, :], first[None, :], 0), axis=1
    )
    same_row = rel_row[:, None] == rel_row[None, :]
    earlier = tile[None, :] < tile[:, None]
    rank = jnp.sum((same_row & earlier).astype(jnp.int32), axis=1)
    mine = jnp.sum(
        jnp.where(rel_row[:, None] == blocks[None, :], base[None, :], 0), axis=1
    )
    pos = mine + rank
    size = nt + nblk * (G - 1) + nchunk * G * U
    size = -(-size // (G * U)) * G * U
    slots = jnp.arange(size, dtype=jnp.int32)
    packed = tile + 1024 * (rel_col + 128 * (rel_row % per_chunk))
    dummy = 1024 * nblk
    listed = jnp.sum(
        jnp.where(slots[:, None] == pos[None, :], (packed - dummy)[None, :], 0), axis=1
    ) + dummy
    return jnp.concatenate([listed, first, steps])


def aggregate(chunk, nchunk, table, hist, tiles):
    nslot, shard, width = len(hist), hist[0].shape[0], hist[0].shape[1]
    block = tiles.shape[1]
    rb = shard // block
    nblk = nslot * rb
    nt = tiles.shape[0]
    per_chunk = nblk // nchunk
    nout = per_chunk // rb
    at = table.shape[0] - 2 * nchunk
    part = nt // NCOPY

    def body(*refs):
        table_s = refs[0]
        hist_refs = refs[1 : 1 + nslot]
        tiles_ref = refs[1 + nslot]
        outs = refs[2 + nslot : 2 + nslot + nout]
        acc, buf, his, sem = refs[2 + nslot + nout :]
        copies = [
            pltpu.make_async_copy(
                tiles_ref.at[pl.ds(c * part, part)], buf.at[pl.ds(c * part, part)], sem.at[c]
            )
            for c in range(NCOPY)
        ]
        for c in copies:
            c.start()
        acc[...] = jnp.zeros_like(acc)
        for s in range(nslot):
            his[s * rb : (s + 1) * rb] = hist_refs[s][...].reshape(rb, block, width)
        his[nblk] = jnp.zeros((block, width), BF16)
        for c in copies:
            c.wait()
        first = table_s[at + chunk]
        steps = table_s[at + nchunk + chunk]

        def step(q, carry):
            parts = []
            rows = []
            for u in range(U):
                start = (first + q) * (G * U) + u * G
                words = [table_s[start + g] for g in range(G)]
                left = jnp.concatenate([buf[w & 1023] for w in words], axis=1)
                right = jnp.concatenate([his[(w >> 10) & 127] for w in words], axis=0)
                rows.append(words[0] >> 17)
                parts.append(jnp.dot(left, right, preferred_element_type=F32))
            for u in range(U):
                acc[rows[u]] += parts[u]
            return carry

        lax.fori_loop(0, steps, step, 0)
        for j in range(nout):
            outs[j][...] = acc[j * rb : (j + 1) * rb].reshape(shard, width).astype(BF16)

    full = pl.BlockSpec((shard, width), lambda i, *_: (0, 0))
    return pl.pallas_call(
        body,
        grid_spec=pltpu.PrefetchScalarGridSpec(
            num_scalar_prefetch=1,
            grid=(1,),
            in_specs=[full] * nslot + [pl.BlockSpec(memory_space=pl.ANY)],
            out_specs=[full] * nout,
            scratch_shapes=[
                pltpu.VMEM((per_chunk, block, width), F32),
                pltpu.VMEM((nt, block, block), BF16),
                pltpu.VMEM((nblk + 1, block, width), BF16),
                pltpu.SemaphoreType.DMA((NCOPY,)),
            ],
        ),
        out_shape=[jax.ShapeDtypeStruct((shard, width), BF16)] * nout,
        compiler_params=pltpu.CompilerParams(vmem_limit_bytes=44 * 2**20),
        name="aggregate",
    )(table, *hist, tiles)


def dense(core, pieces, weight, bias, cotangent):
    rows, width = pieces[0].shape
    half = weight.shape[0] // 2
    n = len(pieces)

    def body(core_s, *refs):
        parts = refs[:n]
        w_ref, b_ref, c_ref, act_ref, keep_ref, send_ref, grad = refs[n:]
        total = parts[0][...].astype(F32)
        for p in parts[1:]:
            total = total + p[...].astype(F32)
        merged = total.astype(BF16)
        pre = jnp.dot(merged, w_ref[...], preferred_element_type=F32) + b_ref[...]
        sig = jax.nn.sigmoid(pre)
        act_ref[...] = (pre * sig).astype(BF16)
        slope = sig * (1.0 + pre * (1.0 - sig))
        masked = (c_ref[...].astype(F32) * slope).astype(BF16)
        grad[...] = lax.dot_general(
            merged, masked, (((0,), (0,)), ((), ())), preferred_element_type=F32
        )
        total_bias = jnp.sum(masked.astype(F32), axis=0, keepdims=True)
        upper = total_bias.astype(BF16).astype(F32)
        lower = total_bias - upper
        line = lax.broadcasted_iota(jnp.int32, (16, width), 0)
        tail = jnp.where(line == 0, upper, jnp.where(line == 1, lower, 0.0)).astype(BF16)
        mine = core_s[0]
        keep_ref[:half] = grad[pl.ds(mine * half, half)].astype(BF16)
        keep_ref[half:] = tail
        send_ref[:half] = grad[pl.ds((1 - mine) * half, half)].astype(BF16)
        send_ref[half:] = tail

    return pl.pallas_call(
        body,
        grid_spec=pltpu.PrefetchScalarGridSpec(
            num_scalar_prefetch=1,
            grid=(1,),
            in_specs=[pl.BlockSpec((rows, width), lambda i, *_: (0, 0))] * n
            + [
                pl.BlockSpec(weight.shape, lambda i, *_: (0, 0)),
                pl.BlockSpec((1, width), lambda i, *_: (0, 0)),
                pl.BlockSpec((rows, width), lambda i, *_: (0, 0)),
            ],
            out_specs=[
                pl.BlockSpec((rows, width), lambda i, *_: (0, 0)),
                pl.BlockSpec((half + 16, width), lambda i, *_: (0, 0)),
                pl.BlockSpec((half + 16, width), lambda i, *_: (0, 0)),
            ],
            scratch_shapes=[pltpu.VMEM(weight.shape, F32)],
        ),
        out_shape=[
            jax.ShapeDtypeStruct((rows, width), BF16),
            jax.ShapeDtypeStruct((half + 16, width), BF16),
            jax.ShapeDtypeStruct((half + 16, width), BF16),
        ],
        compiler_params=pltpu.CompilerParams(vmem_limit_bytes=32 * 2**20),
        name="dense",
    )(core, *pieces, weight, bias.reshape(1, width), cotangent)


def tree_sum(values):
    values = [v.astype(F32) for v in values]
    while len(values) > 1:
        values = [values[i] + values[i + 1] for i in range(0, len(values), 2)]
    return values[0]


def per_device(grp, mem, history, tiles, tile_row, tile_col, weight, bias, cotangent):
    nz = 4
    ny = mem // nz
    nx = grp // 2
    block = tiles.shape[1]
    rb = history.shape[0] // block
    nblk = mem * rb
    me = lax.axis_index("mem").astype(jnp.int32)
    core = (lax.axis_index("grp") % 2).astype(jnp.int32)

    hist = [None] * mem
    hist[0] = history
    for d in (1, 3, 2):
        hist[d * ny] = swap(history, "mem", mem, d * ny)
    for d in (0, 1, 3, 2):
        for j in range(1, ny):
            hist[d * ny + j] = swap(hist[d * ny], "mem", mem, j)

    table = plan(tile_row, tile_col, me, rb, nblk, nz)

    final = []
    for d in (2, 3, 1, 0):
        outs = aggregate(d, nz, table, hist, tiles)
        got = [swap(outs[j], "mem", mem, j) for j in range(1, ny)]
        if d == 0:
            final = [outs[0], *got] + final
        else:
            summed = outs[0].astype(F32)
            for g in got:
                summed = summed + g.astype(F32)
            final.append(swap(summed.astype(BF16), "mem", mem, d * ny))

    activation, keep, send = dense(core.reshape(1), final, weight, bias, cotangent)

    value = tree_sum([keep, swap(send, "grp", grp, 1)]).astype(BF16)
    value = tree_sum([value] + [swap(value, "grp", grp, 2 * d) for d in range(1, nx)]).astype(BF16)
    value = tree_sum([value] + [swap(value, "mem", mem, d) for d in range(1, ny)]).astype(BF16)
    value = tree_sum([value] + [swap(value, "mem", mem, d * ny) for d in range(1, nz)])
    half = weight.shape[0] // 2
    other = swap(value[:half], "grp", grp, 1)
    mine = value[:half]
    weight_grad = jnp.where(
        core == 0, jnp.concatenate([mine, other]), jnp.concatenate([other, mine])
    )
    bias_grad = value[half] + value[half + 1]
    return activation, weight_grad, bias_grad


def solution(mesh):
    rows = P(("grp", "mem"))
    placed = (rows, rows, rows, rows, P(), P(), rows)
    return jax.shard_map(
        functools.partial(per_device, mesh.shape["grp"], mesh.shape["mem"]),
        mesh=mesh,
        in_specs=placed,
        out_specs=(rows, P(), P()),
        check_vma=False,
    )
```

```python
import jax
import jax.numpy as jnp
from jax import lax
from jax.experimental import pallas as pl
from jax.experimental.pallas import tpu as pltpu
from jax.sharding import PartitionSpec as P


NLOAD = 20
ORDER = (2, 3, 1, 0)
G = 4
U = 8
F32 = jnp.float32
BF16 = jnp.bfloat16


def swap(value, axis, size, mask):
    return lax.ppermute(value, axis, [(i, i ^ mask) for i in range(size)])


def plan(row, col, me, rb, nblk, nchunk):
    nt = row.shape[0]
    rel_row = ((row // rb) ^ me) * rb + row % rb
    rel_col = ((col // rb) ^ me) * rb + col % rb
    tile = jnp.arange(nt, dtype=jnp.int32)
    blocks = jnp.arange(nblk, dtype=jnp.int32)
    per_chunk = nblk // nchunk
    counts = jnp.sum((rel_row[None, :] == blocks[:, None]).astype(jnp.int32), axis=1)
    padded = (counts + (G - 1)) // G * G
    same_chunk = (blocks[:, None] // per_chunk) == (blocks[None, :] // per_chunk)
    before = blocks[None, :] < blocks[:, None]
    within = jnp.sum(jnp.where(same_chunk & before, padded[None, :], 0), axis=1)
    chunks = jnp.arange(nchunk, dtype=jnp.int32)
    totals = jnp.sum(
        jnp.where(chunks[:, None] == blocks[None, :] // per_chunk, padded[None, :], 0), axis=1
    )
    steps = (totals + (G * U - 1)) // (G * U)
    first = jnp.sum(jnp.where(chunks[None, :] < chunks[:, None], steps[None, :], 0), axis=1)
    chunk_of = blocks // per_chunk
    base = within + G * U * jnp.sum(
        jnp.where(chunk_of[:, None] == chunks[None, :], first[None, :], 0), axis=1
    )
    same_row = rel_row[:, None] == rel_row[None, :]
    earlier = tile[None, :] < tile[:, None]
    rank = jnp.sum((same_row & earlier).astype(jnp.int32), axis=1)
    mine = jnp.sum(
        jnp.where(rel_row[:, None] == blocks[None, :], base[None, :], 0), axis=1
    )
    pos = mine + rank
    size = nt + nblk * (G - 1) + nchunk * G * U
    size = -(-size // (G * U)) * G * U
    slots = jnp.arange(size, dtype=jnp.int32)
    packed = tile + 1024 * (rel_col + 128 * (rel_row % per_chunk))
    dummy = 1024 * nblk
    listed = jnp.sum(
        jnp.where(slots[:, None] == pos[None, :], (packed - dummy)[None, :], 0), axis=1
    ) + dummy
    return jnp.concatenate([listed, first, steps])


def load(tiles):
    part = tiles.shape[0] // NLOAD

    def body(src, dst, sem):
        copies = [
            pltpu.make_async_copy(
                src.at[pl.ds(c * part, part)], dst.at[pl.ds(c * part, part)], sem.at[c]
            )
            for c in range(NLOAD)
        ]
        for c in copies:
            c.start()
        for c in copies:
            c.wait()

    return pl.pallas_call(
        body,
        in_specs=[pl.BlockSpec(memory_space=pltpu.HBM)],
        out_specs=pl.BlockSpec(memory_space=pltpu.VMEM),
        out_shape=pltpu.VMEM(tiles.shape, tiles.dtype),
        scratch_shapes=[pltpu.SemaphoreType.DMA((NLOAD,))],
        compiler_params=pltpu.CompilerParams(vmem_limit_bytes=4 * 2**20),
        name="load",
    )(tiles)


def aggregate(chunk, nchunk, table, hist, tiles):
    nslot, shard, width = len(hist), hist[0].shape[0], hist[0].shape[1]
    block = tiles.shape[1]
    rb = shard // block
    nblk = nslot * rb
    nt = tiles.shape[0]
    per_chunk = nblk // nchunk
    nout = per_chunk // rb
    at = table.shape[0] - 2 * nchunk

    def body(*refs):
        table_s = refs[0]
        hist_refs = refs[1 : 1 + nslot]
        tiles_ref = refs[1 + nslot]
        outs = refs[2 + nslot : 2 + nslot + nout]
        acc, his = refs[2 + nslot + nout :]
        acc[...] = jnp.zeros_like(acc)
        for s in range(nslot):
            his[s * rb : (s + 1) * rb] = hist_refs[s][...].reshape(rb, block, width)
        his[nblk] = jnp.zeros((block, width), BF16)
        first = table_s[at + chunk]
        steps = table_s[at + nchunk + chunk]

        def step(q, carry):
            parts = []
            rows = []
            for u in range(U):
                start = (first + q) * (G * U) + u * G
                words = [table_s[start + g] for g in range(G)]
                left = jnp.concatenate([tiles_ref[w & 1023] for w in words], axis=1)
                right = jnp.concatenate([his[(w >> 10) & 127] for w in words], axis=0)
                rows.append(words[0] >> 17)
                parts.append(jnp.dot(left, right, preferred_element_type=F32))
            for u in range(U):
                acc[rows[u]] += parts[u]
            return carry

        lax.fori_loop(0, steps, step, 0)
        for j in range(nout):
            outs[j][...] = acc[j * rb : (j + 1) * rb].reshape(shard, width).astype(BF16)

    full = pl.BlockSpec((shard, width), lambda i, *_: (0, 0))
    return pl.pallas_call(
        body,
        grid_spec=pltpu.PrefetchScalarGridSpec(
            num_scalar_prefetch=1,
            grid=(1,),
            in_specs=[full] * nslot + [pl.BlockSpec(memory_space=pltpu.VMEM)],
            out_specs=[full] * nout,
            scratch_shapes=[
                pltpu.VMEM((per_chunk, block, width), F32),
                pltpu.VMEM((nblk + 1, block, width), BF16),
            ],
        ),
        out_shape=[jax.ShapeDtypeStruct((shard, width), BF16)] * nout,
        compiler_params=pltpu.CompilerParams(vmem_limit_bytes=16 * 2**20),
        cost_estimate=pl.CostEstimate(
            flops=2 * nt * block * block * width // nchunk,
            bytes_accessed=nt * block * block * 2 // nchunk,
            transcendentals=0,
        ),
        name="aggregate",
    )(table, *hist, tiles)


def dense(core, pieces, weight, bias, cotangent):
    rows, width = pieces[0].shape
    half = weight.shape[0] // 2
    n = len(pieces)

    def body(core_s, *refs):
        parts = refs[:n]
        w_ref, b_ref, c_ref, act_ref, keep_ref, send_ref, grad = refs[n:]
        total = parts[0][...].astype(F32)
        for p in parts[1:]:
            total = total + p[...].astype(F32)
        merged = total.astype(BF16)
        pre = jnp.dot(merged, w_ref[...], preferred_element_type=F32) + b_ref[...]
        sig = jax.nn.sigmoid(pre)
        act_ref[...] = (pre * sig).astype(BF16)
        slope = sig * (1.0 + pre * (1.0 - sig))
        masked = (c_ref[...].astype(F32) * slope).astype(BF16)
        grad[...] = lax.dot_general(
            merged, masked, (((0,), (0,)), ((), ())), preferred_element_type=F32
        )
        total_bias = jnp.sum(masked.astype(F32), axis=0, keepdims=True)
        upper = total_bias.astype(BF16).astype(F32)
        lower = total_bias - upper
        line = lax.broadcasted_iota(jnp.int32, (16, width), 0)
        tail = jnp.where(line == 0, upper, jnp.where(line == 1, lower, 0.0)).astype(BF16)
        mine = core_s[0]
        keep_ref[:half] = grad[pl.ds(mine * half, half)].astype(BF16)
        keep_ref[half:] = tail
        send_ref[:half] = grad[pl.ds((1 - mine) * half, half)].astype(BF16)
        send_ref[half:] = tail

    return pl.pallas_call(
        body,
        grid_spec=pltpu.PrefetchScalarGridSpec(
            num_scalar_prefetch=1,
            grid=(1,),
            in_specs=[pl.BlockSpec((rows, width), lambda i, *_: (0, 0))] * n
            + [
                pl.BlockSpec(weight.shape, lambda i, *_: (0, 0)),
                pl.BlockSpec((1, width), lambda i, *_: (0, 0)),
                pl.BlockSpec((rows, width), lambda i, *_: (0, 0)),
            ],
            out_specs=[
                pl.BlockSpec((rows, width), lambda i, *_: (0, 0)),
                pl.BlockSpec((half + 16, width), lambda i, *_: (0, 0)),
                pl.BlockSpec((half + 16, width), lambda i, *_: (0, 0)),
            ],
            scratch_shapes=[pltpu.VMEM(weight.shape, F32)],
        ),
        out_shape=[
            jax.ShapeDtypeStruct((rows, width), BF16),
            jax.ShapeDtypeStruct((half + 16, width), BF16),
            jax.ShapeDtypeStruct((half + 16, width), BF16),
        ],
        compiler_params=pltpu.CompilerParams(vmem_limit_bytes=16 * 2**20),
        name="dense",
    )(core, *pieces, weight, bias.reshape(1, width), cotangent)


def tree_sum(values):
    values = [v.astype(F32) for v in values]
    while len(values) > 1:
        values = [values[i] + values[i + 1] for i in range(0, len(values), 2)]
    return values[0]


def per_device(grp, mem, history, tiles, tile_row, tile_col, weight, bias, cotangent):
    nz = 4
    ny = mem // nz
    nx = grp // 2
    block = tiles.shape[1]
    rb = history.shape[0] // block
    nblk = mem * rb
    me = lax.axis_index("mem").astype(jnp.int32)
    core = (lax.axis_index("grp") % 2).astype(jnp.int32)

    hist = [None] * mem
    hist[0] = history
    for d in (1, 3, 2):
        hist[d * ny] = swap(history, "mem", mem, d * ny)
    for d in (0, 1, 3, 2):
        for j in range(1, ny):
            hist[d * ny + j] = swap(hist[d * ny], "mem", mem, j)

    tiles = load(pltpu.with_memory_space_constraint(tiles, pltpu.HBM))
    table = plan(tile_row, tile_col, me, rb, nblk, nz)

    final = []
    for d in ORDER:
        outs = aggregate(d, nz, table, hist, tiles)
        got = [swap(outs[j], "mem", mem, j) for j in range(1, ny)]
        if d == 0:
            final = [outs[0], *got] + final
        else:
            summed = outs[0].astype(F32)
            for g in got:
                summed = summed + g.astype(F32)
            final.append(swap(summed.astype(BF16), "mem", mem, d * ny))

    activation, keep, send = dense(core.reshape(1), final, weight, bias, cotangent)

    value = tree_sum([keep, swap(send, "grp", grp, 1)]).astype(BF16)
    value = tree_sum([value] + [swap(value, "grp", grp, 2 * d) for d in range(1, nx)]).astype(BF16)
    value = tree_sum([value] + [swap(value, "mem", mem, d) for d in range(1, ny)]).astype(BF16)
    value = tree_sum([value] + [swap(value, "mem", mem, d * ny) for d in range(1, nz)])
    half = weight.shape[0] // 2
    other = swap(value[:half], "grp", grp, 1)
    mine = value[:half]
    weight_grad = jnp.where(
        core == 0, jnp.concatenate([mine, other]), jnp.concatenate([other, mine])
    )
    bias_grad = value[half] + value[half + 1]
    return activation, weight_grad, bias_grad


def solution(mesh):
    rows = P(("grp", "mem"))
    placed = (rows, rows, rows, rows, P(), P(), rows)

    def layer(*arrays):
        return per_device(mesh.shape["grp"], mesh.shape["mem"], *arrays)

    return jax.shard_map(
        layer, mesh=mesh, in_specs=placed, out_specs=(rows, P(), P()), check_vma=False
    )
```
